32 devices in a mesh: box: 2 (over y), gx: 8 (over z, x), gy: 2 (over core).
Axes of the slice: x: 2, y: 2, z: 4, core: 2. Of those that a mesh axis runs over, the one named last changes fastest.
Arguments:
- positions: float32 [16, 4, 3, 256], P(('box', 'gx'), 'gy'), parts along dimension 0, may hold values from 0 to 18, as said below
- polarizability: float32 [16, 4, 256], P(('box', 'gx'), 'gy'), parts along dimension 0, may hold values from 0.3 to 1.5
- tile_counts: int32 [16, 4, 2], P(('box', 'gx'), 'gy'), parts along dimension 0, may hold values from 80 to 128, as said below
- molecules: int32 [16, 4, 256], P(('box', 'gx'), 'gy'), parts along dimension 0, may hold values from 0 to 170, as said below
- perm_field: float32 [16, 4, 3, 256], P(('box', 'gx'), 'gy'), parts along dimension 0, may hold values from -6 to 6
- dipoles: float32 [16, 4, 3, 256], P(('box', 'gx'), 'gy'), parts along dimension 0, may hold values from -4 to 4
- past_out: float32 [16, 4, 7, 3, 256], P(('box', 'gx'), 'gy'), parts along dimension 0, may hold values from -4 to 4
- past_res: float32 [16, 4, 7, 3, 256], P(('box', 'gx'), 'gy'), parts along dimension 0, may hold values from -15 to 15
Outputs:
- dipoles_next: float32 [16, 4, 3, 256], P(('box', 'gx'), 'gy'), parts along dimension 0
- diis_weights: float32 [16], P('box'), parts along dimension 0
The draws below stay inside these ranges and needn't reach their ends.
There are 2 independent parts, one for each index of `box`. The reference program is written for one: setup_inputs(seed, part) draws one part's arguments, and reference() takes and returns one part's arrays. A program takes and returns all parts, laid end to end along the dimension named above; each array names one. Nothing has to cross between parts.
Inputs may be any that keep to these rules, and one draw needn't show every extreme that they name: x and y in [0, 9); z of an atom in z-tile t lies in [9 t, 9 t + 9); padded slots carry positions too. `tile_counts`: some z-tile is full. `molecules`: a group holds at most three atoms, all of one z-tile of one cell.
All inputs are finite; a program needn't handle non-finite values.
Results may differ from the reference program's by a relative error of at most 0.0003.
Values sent between devices are 32-bit elements; how exact they have to be, the bound alone decides.
A program may use at most 64 MiB of HBM per device.

```python
import math
import jax
import jax.numpy as jnp
from jax import lax

TILE = 128
TILES = 2
HIST = 8
ITERS = 2
ATOMS = 256
CX = 8
CY = 4


def draw_positions(key, part):
    key_plane, key_height = jax.random.split(jax.random.fold_in(key, 11))
    plane_xy = jax.random.uniform(key_plane, (CX, CY, 2, ATOMS), jnp.float32, 0.0, 9.0)
    height = jax.random.uniform(key_height, (CX, CY, 1, ATOMS), jnp.float32, 0.0, 9.0)
    floor_z = (lax.broadcasted_iota(jnp.int32, (CX, CY, 1, ATOMS), 3) // TILE).astype(jnp.float32) * 9.0
    return jnp.concatenate([plane_xy, height + floor_z], axis=2)


def draw_tile_counts(key, part):
    key_fill, key_full = jax.random.split(jax.random.fold_in(key, 23))
    counts = jax.random.randint(key_fill, (CX * CY * TILES,), TILE - 3 * TILE // 8, TILE + 1)
    full_at = jax.random.randint(key_full, (), 0, CX * CY * TILES)
    return counts.at[full_at].set(TILE).reshape(CX, CY, TILES).astype(jnp.int32)


def draw_molecules(key, part):
    dims_all = (CX, CY, TILES, TILE)
    scores = jax.random.randint(jax.random.fold_in(key, 37), dims_all, 0, 1 << 20)
    scores = scores * TILE + lax.broadcasted_iota(jnp.int32, dims_all, 3)
    shuffled = jnp.argsort(scores, axis=3, stable=True).astype(jnp.int32)
    tile_base = lax.broadcasted_iota(jnp.int32, dims_all, 2) * TILE
    return (tile_base + shuffled // 3).reshape(CX, CY, ATOMS)


def draw_past_res(key, part):
    key_private = jax.random.fold_in(jax.random.fold_in(key, 41), 0)
    dims_all = (CX, CY, HIST - 1, 3, ATOMS)
    along_x = lax.broadcasted_iota(jnp.float32, dims_all, 0) / max(CX - 1, 1)
    values = 3.0 ** along_x * jnp.clip(jax.random.normal(key_private, dims_all, jnp.float32), -4.0, 4.0)
    return jnp.clip(values, -15.0, 15.0)


def block_levels(stream_key, shape, cuts, least, high):
    level = 1.0
    for dim, parts in cuts:
        steps = jax.random.uniform(jax.random.fold_in(jax.random.fold_in(stream_key, 6), dim), (parts,), jnp.float32, least / len(cuts), high / len(cuts))
        level = level * jnp.repeat(jnp.exp(steps), shape[dim] // parts).reshape((-1,) + (1,) * (len(shape) - 1 - dim))
    return level


def gaussian(own_key, dims, spread, most, cuts=(), held_as=jnp.bfloat16):
    values = spread * jax.random.normal(own_key, dims, jnp.float32)
    if cuts:
        values = values * block_levels(own_key, dims, cuts, -0.22, 0.18)
    return jnp.clip(values, -most, most).astype(held_as)


def setup_inputs(seed: int = 0, part: int = 0) -> dict:
    seeds = jax.random.split(jax.random.key(seed), 9)
    part_splits = jax.random.split(jax.random.fold_in(seeds[8], part), 9)
    return {
        "positions": draw_positions(jax.random.fold_in(jax.random.fold_in(seeds[8], part), 71), part),
        "polarizability": jnp.clip(jnp.exp(math.log(1.5) - 1.60943787 * jax.random.uniform(part_splits[1], (CX, CY, ATOMS), jnp.float32) ** block_levels(part_splits[1], (CX, CY, ATOMS), ((0, 8), (1, 2)), -0.2, 0.2)), 0.3, 1.5),
        "tile_counts": draw_tile_counts(jax.random.fold_in(jax.random.fold_in(seeds[8], part), 71), part),
        "molecules": draw_molecules(jax.random.fold_in(jax.random.fold_in(seeds[8], part), 71), part),
        "perm_field": gaussian(part_splits[4], (CX, CY, 3, ATOMS), 1.0, 6.0, ((0, 8), (1, 2)), jnp.float32),
        "dipoles": gaussian(part_splits[5], (CX, CY, 3, ATOMS), 0.5, 4.0, ((0, 8), (1, 2)), jnp.float32),
        "past_out": gaussian(part_splits[6], (CX, CY, HIST - 1, 3, ATOMS), 0.5, 4.0, ((0, 8), (1, 2)), jnp.float32),
        "past_res": draw_past_res(jax.random.fold_in(jax.random.fold_in(seeds[8], part), 71), part),
    }


CELL_SIDE = 9.0
CUTOFF_SQ = 81.0
SOFTENING = 0.25
THOLE_DAMP = 0.39
FAR_LIFT = 1000.0

def pair_terms(target_coords, target_polar, target_groups, target_occupied, source_coords, source_polar, source_groups, source_occupied):
    displace = source_coords[:, None, :] - target_coords[:, :, None]
    square_dist = lax.optimization_barrier(jnp.sum(displace * displace, axis=0)) + SOFTENING
    distance = jnp.sqrt(square_dist)
    cube_dist = square_dist * distance
    damped = THOLE_DAMP * cube_dist / jnp.sqrt(target_polar[:, None] * source_polar[None, :])
    damping = jnp.exp(-damped)
    tapering = jnp.square(jnp.maximum(1.0 - square_dist / CUTOFF_SQ, 0.0))
    keeper = (target_groups[:, None] != source_groups[None, :]).astype(jnp.float32)
    weight = tapering * keeper * target_occupied[:, None] * source_occupied[None, :]
    isotropic = weight * -jnp.expm1(-damped) / cube_dist
    tensorial = 3.0 * weight * (1.0 - (1.0 + damped) * damping) / (cube_dist * square_dist)
    return (displace, isotropic, tensorial)

def field_targets(displace, isotropic, tensorial, source_dipole):
    projected = lax.optimization_barrier(jnp.sum(displace * source_dipole[:, None, :], axis=0))
    return lax.optimization_barrier(jnp.sum(displace * (tensorial * projected)[None], axis=2)) - lax.optimization_barrier(jnp.sum(isotropic[None] * source_dipole[:, None, :], axis=2))

def tiled(values, filler, tile_count):
    shaped = values.reshape(values.shape[:-1] + (tile_count, values.shape[-1] // tile_count))
    widths = [(0, 0)] * (shaped.ndim - 2) + [(1, 1), (0, 0)]
    return jnp.pad(shaped, widths, constant_values=filler)

def padded_coords(coords, tile_count):
    marker = tiled(jnp.zeros_like(coords), 1.0, tile_count)
    lifted = jnp.array([0.0, 0.0, FAR_LIFT], jnp.float32).reshape(3, 1, 1)
    return tiled(coords, 0.0, tile_count) + marker * lifted

def band_sources(padded, tile_at):
    coords, polarity, groups, occupied, dipole = padded

    def flat_vector(member):
        window_part = lax.dynamic_slice_in_dim(member, tile_at, 3, 2)
        return jnp.transpose(window_part, (1, 0, 2, 3)).reshape(3, -1)

    def flat_scalar(member):
        return lax.dynamic_slice_in_dim(member, tile_at, 3, 1).reshape(-1)
    return (flat_vector(coords), flat_scalar(polarity), flat_scalar(groups), flat_scalar(occupied), flat_vector(dipole))

def band_field(own_cell, padded, tile_count):
    coords, polarity, groups, occupied = own_cell
    tile_width = coords.shape[-1] // tile_count

    def one_tile(tile_at):
        first_slot = tile_at * tile_width
        source_coords, source_polar, source_groups, source_occupied, source_dipole = band_sources(padded, tile_at)
        displace, isotropic, tensorial = pair_terms(lax.dynamic_slice_in_dim(coords, first_slot, tile_width, 1), lax.dynamic_slice_in_dim(polarity, first_slot, tile_width, 0), lax.dynamic_slice_in_dim(groups, first_slot, tile_width, 0), lax.dynamic_slice_in_dim(occupied, first_slot, tile_width, 0), source_coords, source_polar, source_groups, source_occupied)
        return field_targets(displace, isotropic, tensorial, source_dipole)
    fields = lax.map(one_tile, jnp.arange(tile_count, dtype=jnp.int32))
    return jnp.transpose(fields, (1, 0, 2)).reshape(3, -1)

def field_on(positions, polarizability, molecules, occupied, dipole):
    gathered = ([], [], [], [], [])
    for shift_x in (-1, 0, 1):
        for shift_y in (-1, 0, 1):

            def rolled(values):
                return jnp.roll(values, (-shift_x, -shift_y), axis=(0, 1))
            lifted = jnp.array([CELL_SIDE * shift_x, CELL_SIDE * shift_y, 0.0], jnp.float32).reshape(3, 1)
            gathered[0].append(rolled(positions) + lifted)
            gathered[1].append(rolled(polarizability))
            if shift_x == 0 and shift_y == 0:
                gathered[2].append(molecules)
            else:
                gathered[2].append(jnp.full_like(molecules, -1))
            gathered[3].append(rolled(occupied))
            gathered[4].append(rolled(dipole))
    padded = (padded_coords(jnp.stack(gathered[0], 2), TILES), tiled(jnp.stack(gathered[1], 2), 1.0, TILES), tiled(jnp.stack(gathered[2], 2), -1, TILES), tiled(jnp.stack(gathered[3], 2), 0.0, TILES), tiled(jnp.stack(gathered[4], 2), 0.0, TILES))
    cell_total = CX * CY
    flat_padded = tuple((member.reshape((cell_total,) + member.shape[2:]) for member in padded))
    flat_own = tuple((member.reshape((cell_total,) + member.shape[2:]) for member in (positions, polarizability, molecules, occupied)))

    def per_cell(both_parts):
        return band_field(both_parts[0], both_parts[1], TILES)
    fields = lax.map(per_cell, (flat_own, flat_padded))
    return fields.reshape(CX, CY, 3, -1)

def diis_weights(gram_matrix):
    lower = jnp.linalg.cholesky(gram_matrix)
    history = gram_matrix.shape[0]
    forward = []
    for row_at in range(history):
        running = jnp.ones((), gram_matrix.dtype)
        for col_at in range(row_at):
            running = running - lower[row_at, col_at] * forward[col_at]
        forward.append(running / lower[row_at, row_at])
    backward = [None] * history
    for row_at in reversed(range(history)):
        running = forward[row_at]
        for col_at in range(row_at + 1, history):
            running = running - lower[col_at, row_at] * backward[col_at]
        backward[row_at] = running / lower[row_at, row_at]
    solved = jnp.stack(backward)
    return solved / jnp.sum(solved)

def reference(positions, polarizability, tile_counts, molecules, perm_field, dipoles, past_out, past_res):
    slot_index = lax.broadcasted_iota(jnp.int32, (CX, CY, TILES, TILE), 3)
    occupied = (slot_index < tile_counts[:, :, :, None]).astype(jnp.float32).reshape(CX, CY, ATOMS)
    occupied_vec = occupied[:, :, None, :]
    current = dipoles * occupied_vec
    stored_out = jnp.moveaxis(past_out, 2, 0) * occupied_vec
    stored_res = jnp.moveaxis(past_res, 2, 0) * occupied_vec
    scaled = (polarizability * occupied)[:, :, None, :]
    weights = jnp.zeros((HIST,), jnp.float32)
    for step_at in range(ITERS):
        induced = field_on(positions, polarizability, molecules, occupied, current)
        jacobi = scaled * (perm_field + induced)
        residual = jacobi - current
        outputs_all = jnp.concatenate([stored_out, jacobi[None]], 0)
        residual_all = jnp.concatenate([stored_res, residual[None]], 0)
        flattened = residual_all.reshape(HIST, -1)
        gram_matrix = jnp.dot(flattened.astype(jnp.float32), flattened.T.astype(jnp.float32), precision=lax.Precision.HIGHEST, preferred_element_type=jnp.float32)
        weights = diis_weights(gram_matrix)
        current = lax.optimization_barrier(jnp.sum(weights[:, None, None, None, None] * outputs_all, axis=0))
        stored_out = outputs_all[1:]
        stored_res = residual_all[1:]
    return (current, weights)
```

```python
import functools

import jax
import jax.numpy as jnp
from jax import lax
from jax.experimental import pallas as pl
from jax.experimental.pallas import tpu as pltpu
from jax.sharding import PartitionSpec as P

CELL_SIDE = 9.0
CUTOFF_SQ = 81.0
SOFTENING = 0.25
THOLE_DAMP = 0.39
LANES = 128
SUBLANES = 8
ROWS = 32
MESH = pl.DeviceIdType.MESH

BLOCKS = ((0, 0), (0, 1), (1, 0), (1, 1), (-1, 0), (-1, 1))
PHASES = ((0,), (1,), (2, 3), (4, 5))


def block_row(cell, half, cells):
    if half == 0:
        return cell
    return -1 if cell == cells - 1 else cells


def sources(target_cell, blocks, cells, tiles):
    found = []
    for block in blocks:
        x_offset, half = BLOCKS[block]
        for cell in range(cells):
            if half == 1 and cell not in (0, cells - 1):
                continue
            if abs(block_row(cell, half, cells) - target_cell) > 1:
                continue
            for tile in range(tiles):
                found.append((block, cell, tile, block == 0 and cell == target_cell))
    return found


def kernel(
    nx,
    ny,
    cells,
    slots,
    stat_ref,
    out_hist,
    res_hist,
    own_ref,
    next_ref,
    weight_ref,
    stat_halo,
    hist_halo,
    jac_halo,
    src,
    tgt,
    iso,
    ten,
    acc,
    jac_own,
    vec,
    gram_send,
    gram_recv,
    stat_send_sem,
    stat_recv_sem,
    hist_send_sem,
    hist_recv_sem,
    jac_send_sem,
    jac_recv_sem,
    gram_send_sem,
    gram_recv_sem,
):
    tiles = slots // LANES
    width = cells * 3 * slots
    total = nx * ny
    my_x = lax.axis_index("gx")
    my_y = lax.axis_index("gy")
    me = my_x * ny + my_y

    def other(step):
        flat = lax.rem(me + step, total)
        return {"gx": flat // ny, "gy": lax.rem(flat, ny)}

    barrier = pltpu.get_barrier_semaphore()

    def greet(step, carry):
        pl.semaphore_signal(barrier, inc=1, device_id=other(step), device_id_type=MESH)
        return carry

    lax.fori_loop(1, total, greet, 0)
    pl.semaphore_wait(barrier, total - 1)

    def halo_copies(source, landing, send_sem, recv_sem):
        copies = []
        for at, (x_offset, half) in enumerate(BLOCKS[1:]):
            target = {
                "gx": lax.rem(my_x - x_offset + nx, nx),
                "gy": lax.rem(my_y + half, ny),
            }
            copies.append(
                pltpu.make_async_remote_copy(
                    src_ref=source,
                    dst_ref=landing.at[at],
                    send_sem=send_sem.at[at],
                    recv_sem=recv_sem.at[at],
                    device_id=target,
                    device_id_type=MESH,
                )
            )
        return copies

    stat_copies = halo_copies(stat_ref, stat_halo, stat_send_sem, stat_recv_sem)
    hist_copies = halo_copies(out_hist, hist_halo, hist_send_sem, hist_recv_sem)
    for copy in stat_copies:
        copy.start()
    for copy in hist_copies:
        copy.start()

    def prepare(block, stat):
        x_offset, half = BLOCKS[block]
        row = lax.broadcasted_iota(jnp.int32, (SUBLANES, slots), 0)
        for cell in range(cells):
            span = slice(cell * slots, (cell + 1) * slots)
            shift_y = CELL_SIDE * block_row(cell, half, cells)
            lift = jnp.where(row == 0, CELL_SIDE * x_offset, jnp.where(row == 1, shift_y, 0.0))
            src[block, :, span] = stat[:, span] + lift

    prepare(0, stat_ref)
    for cell in range(cells):
        span = slice(cell * slots, (cell + 1) * slots)
        columns = jnp.transpose(stat_ref[:, span])
        for at, (row, scale, shift) in enumerate(
            (
                (0, 1.0, 0.0),
                (1, 1.0, CELL_SIDE * cell),
                (2, 1.0, 0.0),
                (3, -THOLE_DAMP, 0.0),
                (7, 1.0, 0.0),
            )
        ):
            column = columns[:, row : row + 1] * scale + shift
            tgt[at, span, :] = jnp.broadcast_to(column, (slots, LANES))

    sub = lax.broadcasted_iota(jnp.int32, (SUBLANES, LANES), 0)
    lane = lax.broadcasted_iota(jnp.int32, (SUBLANES, LANES), 1)
    chunks = [slice(at * LANES, (at + 1) * LANES) for at in range(width // LANES)]

    def inner(rows, vector):
        parts = [r * v for r, v in zip(rows, vector)]
        while len(parts) > 1:
            parts = [sum(parts[at : at + 2]) for at in range(0, len(parts), 2)]
        return jnp.sum(parts[0], axis=1, keepdims=True)

    hist_rows = [res_hist[:, chunk] for chunk in chunks]
    past_gram = jnp.zeros((SUBLANES, LANES), jnp.float32)
    for k in range(SUBLANES - 1):
        column = inner(hist_rows, [rows[k : k + 1] for rows in hist_rows])
        past_gram = past_gram + jnp.where(lane == k, column, 0.0)

    tile_index = [
        {key[:3]: at for at, key in enumerate(sources(c, range(len(BLOCKS)), cells, tiles))}
        for c in range(cells)
    ]

    def first_field(phase, first):
        for c in range(cells):
            met = sources(c, phase, cells, tiles)

            def group(step, carry, c=c, met=met):
                local = pl.ds(pl.multiple_of(step * ROWS, ROWS), ROWS)
                at_slot = pl.ds(pl.multiple_of(c * slots + step * ROWS, ROWS), ROWS)
                ax, ay, az, an = (tgt[m, at_slot, :] for m in range(4))
                if first:
                    sums = [jnp.zeros((ROWS, LANES), jnp.float32)] * 3
                else:
                    sums = [acc[c, m, local, :] for m in range(3)]
                for block, cell, tile, same in met:
                    span = slice(cell * slots + tile * LANES, cell * slots + (tile + 1) * LANES)
                    bx, by, bz, bn, vx, vy, vz, bm = (
                        src[block, m : m + 1, span] for m in range(8)
                    )
                    dx, dy, dz = bx - ax, by - ay, bz - az
                    s = dx * dx + dy * dy + dz * dz + SOFTENING
                    inv = lax.rsqrt(s)
                    inv2 = inv * inv
                    inv3 = inv2 * inv
                    minus_x = (s * s) * inv * (an * bn)
                    e = jnp.exp(minus_x)
                    t = jnp.maximum(1.0 - s * (1.0 / CUTOFF_SQ), 0.0)
                    w = t * t * inv3
                    if same:
                        w = jnp.where(tgt[4, at_slot, :] != bm, w, 0.0)
                    rest = 1.0 - e
                    iso_v = w * rest
                    ten_v = w * (3.0 * inv2) * (rest + minus_x * e)
                    where = tile_index[c][(block, cell, tile)]
                    iso[c, where, local, :] = iso_v
                    ten[c, where, local, :] = ten_v
                    q = ten_v * (dx * vx + dy * vy + dz * vz)
                    sums = [
                        sums[0] + (dx * q - iso_v * vx),
                        sums[1] + (dy * q - iso_v * vy),
                        sums[2] + (dz * q - iso_v * vz),
                    ]
                for m in range(3):
                    acc[c, m, local, :] = sums[m]
                return carry

            lax.fori_loop(0, slots // ROWS, group, 0)

    def second_field():
        for c in range(cells):
            met = sources(c, range(len(BLOCKS)), cells, tiles)

            def group(step, carry, c=c, met=met):
                local = pl.ds(pl.multiple_of(step * ROWS, ROWS), ROWS)
                at_slot = pl.ds(pl.multiple_of(c * slots + step * ROWS, ROWS), ROWS)
                ax, ay, az = (tgt[m, at_slot, :] for m in range(3))
                sums = [jnp.zeros((ROWS, LANES), jnp.float32)] * 3
                for block, cell, tile, _ in met:
                    first = cell * slots + tile * LANES
                    bx, by, bz = (src[block, m : m + 1, first : first + LANES] for m in range(3))
                    starts = [(cell * 3 + m) * slots + tile * LANES for m in range(3)]
                    vx, vy, vz = (vec[block : block + 1, at : at + LANES] for at in starts)
                    dx, dy, dz = bx - ax, by - ay, bz - az
                    where = tile_index[c][(block, cell, tile)]
                    iso_v = iso[c, where, local, :]
                    q = ten[c, where, local, :] * (dx * vx + dy * vy + dz * vz)
                    sums = [
                        sums[0] + (dx * q - iso_v * vx),
                        sums[1] + (dy * q - iso_v * vy),
                        sums[2] + (dz * q - iso_v * vz),
                    ]
                for m in range(3):
                    acc[c, m, local, :] = sums[m]
                return carry

            lax.fori_loop(0, slots // ROWS, group, 0)

    def jacobi_rows():
        found = []
        for c in range(cells):
            for m in range(3):
                for tile in range(tiles):
                    part = acc[c, m, tile * LANES : (tile + 1) * LANES, :]
                    field = jnp.sum(jnp.transpose(part), axis=0, keepdims=True)
                    chunk = chunks[len(found)]
                    found.append(own_ref[0:1, chunk] * (own_ref[1:2, chunk] + field))
        return found

    def gram_share(turn, mine):
        gram_send[turn] = mine

        def copy_to(step):
            return pltpu.make_async_remote_copy(
                src_ref=gram_send.at[turn],
                dst_ref=gram_recv.at[turn, step - 1],
                send_sem=gram_send_sem.at[turn],
                recv_sem=gram_recv_sem.at[turn],
                device_id=other(step),
                device_id_type=MESH,
            )

        def send(step, carry):
            copy_to(step).start()
            return carry

        lax.fori_loop(1, total, send, 0)

        def finish():
            landed = gram_recv.at[turn]
            pltpu.make_async_copy(landed, landed, gram_recv_sem.at[turn]).wait()
            summed = mine + jnp.sum(gram_recv[turn], axis=0)
            return summed

        def sent():
            left = gram_recv.at[turn]
            pltpu.make_async_copy(left, left, gram_send_sem.at[turn]).wait()

        return finish, sent

    def mirrored(gram, column, k):
        row = jnp.sum(jnp.where(sub == lane, column, 0.0), axis=0, keepdims=True)
        return jnp.where(lane == k, column, jnp.where(sub == k, row, gram))

    def solve(gram):
        held = jnp.where(lane == SUBLANES, 1.0, gram)
        for k in range(SUBLANES):
            column = jnp.broadcast_to(held[:, k : k + 1], held.shape)
            pivot_row = held[k : k + 1, :] / column[k : k + 1, :]
            held = jnp.where(sub == k, pivot_row, held - column * pivot_row)
        y = jnp.broadcast_to(held[:, SUBLANES : SUBLANES + 1], held.shape)
        return y / jnp.sum(y, axis=0, keepdims=True)

    def mixed(hist, weights, chunk):
        return jnp.sum(weights * hist, axis=0, keepdims=True)

    newest = SUBLANES - 1
    for at, phase in enumerate(PHASES):
        for block in phase:
            if block:
                stat_copies[block - 1].wait_recv()
                prepare(block, stat_halo.at[block - 1])
        first_field(phase, at == 0)

    jacobi = jacobi_rows()
    for row, chunk in zip(jacobi, chunks):
        jac_own[0:1, chunk] = row
    jac_copies = halo_copies(jac_own, jac_halo, jac_send_sem, jac_recv_sem)
    residual = []
    for at, chunk in enumerate(chunks):
        cell, rest = divmod(at, 3 * tiles)
        m, tile = divmod(rest, tiles)
        first = cell * slots + tile * LANES
        residual.append(jacobi[at] - stat_ref[4 + m : 5 + m, first : first + LANES])
    res_rows = [jnp.where(sub == newest, r, rows) for r, rows in zip(residual, hist_rows)]
    column = inner(res_rows, residual)
    finish, first_sent = gram_share(0, jnp.where(lane == newest, column, past_gram))
    for copy in jac_copies:
        copy.start()
    gram = finish()
    gram = mirrored(gram, jnp.broadcast_to(gram[:, newest : newest + 1], gram.shape), newest)
    weights = solve(gram)

    current = []
    for at, chunk in enumerate(chunks):
        row = mixed(out_hist[:, chunk], weights, chunk) + weights[newest : newest + 1] * jacobi[at]
        current.append(row)
        vec[0:1, chunk] = row
    for block in range(1, len(BLOCKS)):
        hist_copies[block - 1].wait_recv()
        jac_copies[block - 1].wait_recv()
        for chunk in chunks:
            vec[block : block + 1, chunk] = (
                mixed(hist_halo[block - 1, :, chunk], weights, chunk)
                + weights[newest : newest + 1] * jac_halo[block - 1, 0:1, chunk]
            )
    second_field()

    jacobi_next = jacobi_rows()
    residual = [a - b for a, b in zip(jacobi_next, current)]
    res_rows = [jnp.where(sub == 0, r, rows) for r, rows in zip(residual, res_rows)]
    column = inner(res_rows, residual)
    finish, second_sent = gram_share(1, jnp.broadcast_to(column, (SUBLANES, LANES)))
    gram = mirrored(gram, finish(), 0)
    weights = solve(gram)
    kept = jnp.where(sub == 0, 0.0, weights)
    for at, chunk in enumerate(chunks):
        cell, rest = divmod(at, 3 * tiles)
        m, tile = divmod(rest, tiles)
        next_ref[0, cell, m : m + 1, tile * LANES : (tile + 1) * LANES] = (
            mixed(out_hist[:, chunk], kept, chunk)
            + weights[newest : newest + 1] * jac_own[0:1, chunk]
            + weights[0:1] * jacobi_next[at]
        )
    weight_ref[0:newest, :] = weights[1:]
    weight_ref[newest:, :] = weights[0:1]

    for copy in stat_copies + hist_copies + jac_copies:
        copy.wait_send()
    first_sent()
    second_sent()


def body(nx, ny, positions, polarizability, tile_counts, molecules, perm_field, dipoles, past_out, past_res):
    cells, tile_count = tile_counts.shape[1:]
    slots = positions.shape[-1]
    tile_width = slots // tile_count
    tiles = slots // LANES
    past = past_out.shape[2]
    assert ny == 2 and nx > 2 and cells > 1 and past + 1 == SUBLANES and slots % LANES == 0
    index = lax.broadcasted_iota(jnp.int32, (cells, tile_count, tile_width), 2)
    occupied = (index < tile_counts[0][:, :, None]).astype(jnp.float32).reshape(cells, slots)
    spread = occupied[:, None, :]
    static = jnp.concatenate(
        [
            positions[0],
            lax.rsqrt(polarizability[0])[:, None],
            dipoles[0] * spread,
            molecules[0].astype(jnp.float32)[:, None],
        ],
        axis=1,
    )
    static = jnp.moveaxis(static, 1, 0).reshape(SUBLANES, cells * slots)
    width = cells * 3 * slots

    def history(stored):
        rows = jnp.moveaxis(stored[0] * spread[:, None], 1, 0).reshape(past, width)
        return jnp.pad(rows, ((0, SUBLANES - past), (0, 0)))

    scaled = jnp.broadcast_to((polarizability[0] * occupied)[:, None], (cells, 3, slots))
    own = jnp.stack([scaled.reshape(width), perm_field[0].reshape(width)])

    halo = len(BLOCKS) - 1
    met = len(sources(0, range(len(BLOCKS)), cells, tiles))
    vmem = pl.BlockSpec(memory_space=pltpu.VMEM)
    pairs_kept = cells * slots * met * LANES
    current, weights = pl.pallas_call(
        functools.partial(kernel, nx, ny, cells, slots),
        out_shape=(
            jax.ShapeDtypeStruct((1, cells, 3, slots), jnp.float32),
            jax.ShapeDtypeStruct((SUBLANES, LANES), jnp.float32),
        ),
        in_specs=[vmem] * 4,
        out_specs=(vmem, vmem),
        scratch_shapes=[
            pltpu.VMEM((halo, SUBLANES, cells * slots), jnp.float32),
            pltpu.VMEM((halo, SUBLANES, width), jnp.float32),
            pltpu.VMEM((halo, 1, width), jnp.float32),
            pltpu.VMEM((halo + 1, SUBLANES, cells * slots), jnp.float32),
            pltpu.VMEM((5, cells * slots, LANES), jnp.float32),
            pltpu.VMEM((cells, met, slots, LANES), jnp.float32),
            pltpu.VMEM((cells, met, slots, LANES), jnp.float32),
            pltpu.VMEM((cells, 3, slots, LANES), jnp.float32),
            pltpu.VMEM((1, width), jnp.float32),
            pltpu.VMEM((SUBLANES, width), jnp.float32),
            pltpu.VMEM((2, SUBLANES, LANES), jnp.float32),
            pltpu.VMEM((2, nx * ny - 1, SUBLANES, LANES), jnp.float32),
            pltpu.SemaphoreType.DMA((halo,)),
            pltpu.SemaphoreType.DMA((halo,)),
            pltpu.SemaphoreType.DMA((halo,)),
            pltpu.SemaphoreType.DMA((halo,)),
            pltpu.SemaphoreType.DMA((halo,)),
            pltpu.SemaphoreType.DMA((halo,)),
            pltpu.SemaphoreType.DMA((2,)),
            pltpu.SemaphoreType.DMA((2,)),
        ],
        compiler_params=pltpu.CompilerParams(
            collective_id=0, has_side_effects=True, vmem_limit_bytes=48 * 1024 * 1024
        ),
        cost_estimate=pl.CostEstimate(
            flops=70 * pairs_kept, bytes_accessed=16 * width * SUBLANES, transcendentals=2 * pairs_kept
        ),
    )(static, history(past_out), history(past_res), own)
    return (current, weights[:, 0])


def solution(mesh):
    cell_axes = P(("box", "gx"), "gy")
    return jax.shard_map(
        functools.partial(body, mesh.shape["gx"], mesh.shape["gy"]),
        mesh=mesh,
        in_specs=(cell_axes,) * 8,
        out_specs=(cell_axes, P("box")),
        check_vma=False,
    )
```

```python
import functools

import jax
import jax.numpy as jnp
from jax import lax
from jax.experimental import pallas as pl
from jax.experimental.pallas import tpu as pltpu
from jax.sharding import PartitionSpec as P

CELL_SIDE = 9.0
CUTOFF_SQ = 81.0
SOFTENING = 0.25
THOLE_DAMP = 0.39
LANES = 128
SUBLANES = 8
ROWS = 32
MESH = pl.DeviceIdType.MESH

BLOCKS = ((0, 0), (0, 1), (1, 0), (1, 1), (-1, 0), (-1, 1))
PHASES = ((0,), (1,), (2, 3), (4, 5))


def block_row(cell, half, cells):
    if half == 0:
        return cell
    return -1 if cell == cells - 1 else cells


def sources(target_cell, blocks, cells, tiles):
    found = []
    for block in blocks:
        x_offset, half = BLOCKS[block]
        for cell in range(cells):
            if half == 1 and cell not in (0, cells - 1):
                continue
            if abs(block_row(cell, half, cells) - target_cell) > 1:
                continue
            for tile in range(tiles):
                found.append((block, cell, tile, block == 0 and cell == target_cell))
    return found


def kernel(
    nx,
    ny,
    cells,
    slots,
    tile_width,
    counts,
    args,
    outs,
    held,
    stat,
    out_hist,
    res_hist,
    scale,
    stat_halo,
    hist_halo,
    jac_halo,
    src,
    tgt,
    pair,
    acc,
    jac_own,
    vec,
    past_send,
    past_recv,
    row_send,
    row_recv,
    in_sem,
    stat_sem,
    hist_sem,
    jac_sem,
    past_sem,
    row_sem,
):
    next_ref, weight_ref = outs
    positions, polarity, molecules, permanent, dipoles, past_out, past_res = held
    tiles = slots // LANES
    width = cells * 3 * slots
    total = nx * ny
    my_x = lax.axis_index("gx")
    my_y = lax.axis_index("gy")
    me = my_x * ny + my_y

    def other(step):
        flat = lax.rem(me + step, total)
        return {"gx": flat // ny, "gy": lax.rem(flat, ny)}

    barrier = pltpu.get_barrier_semaphore()

    def greet(step, carry):
        pl.semaphore_signal(barrier, inc=1, device_id=other(step), device_id_type=MESH)
        return carry

    lax.fori_loop(1, total, greet, 0)
    fetches = [
        pltpu.make_async_copy(arg.at[0], into, in_sem.at[at])
        for at, (arg, into) in enumerate(zip(args, held))
    ]
    for fetch in fetches:
        fetch.start()

    def halo_copies(source, landing, sems):
        copies = []
        for at, (x_offset, half) in enumerate(BLOCKS[1:]):
            target = {
                "gx": lax.rem(my_x - x_offset + nx, nx),
                "gy": lax.rem(my_y + half, ny),
            }
            copies.append(
                pltpu.make_async_remote_copy(
                    src_ref=source,
                    dst_ref=landing.at[at],
                    send_sem=sems.at[0, at],
                    recv_sem=sems.at[1, at],
                    device_id=target,
                    device_id_type=MESH,
                )
            )
        return copies

    index = lax.broadcasted_iota(jnp.int32, (1, slots), 1)
    occupied = []
    for cell in range(cells):
        live = jnp.zeros((1, slots), jnp.float32)
        for tile in range(slots // tile_width):
            first = tile * tile_width
            inside = jnp.logical_and(index >= first, index < first + counts[0, cell, tile])
            live = jnp.where(inside, 1.0, live)
        occupied.append(live)

    for fetch in fetches:
        fetch.wait()
    for cell in range(cells):
        span = slice(cell * slots, (cell + 1) * slots)
        polar = polarity[cell : cell + 1, :]
        for m in range(3):
            stat[m : m + 1, span] = positions[m, cell : cell + 1, :]
            stat[4 + m : 5 + m, span] = dipoles[m, cell : cell + 1, :] * occupied[cell]
        stat[3:4, span] = lax.rsqrt(polar)
        stat[7:8, span] = molecules[cell : cell + 1, :].astype(jnp.float32)
        scale[0:1, span] = polar * occupied[cell]
    pl.semaphore_wait(barrier, total - 1)
    stat_copies = halo_copies(stat, stat_halo, stat_sem)
    for copy in stat_copies:
        copy.start()

    for stored, hist in ((past_res, res_hist), (past_out, out_hist)):
        hist[SUBLANES - 1 :, :] = jnp.zeros((1, width), jnp.float32)
        for cell in range(cells):
            for m in range(3):
                first = (cell * 3 + m) * slots
                for k in range(SUBLANES - 1):
                    row = stored[k, m, cell : cell + 1, :] * occupied[cell]
                    hist[k : k + 1, first : first + slots] = row

    def prepare(block, block_stat):
        x_offset, half = BLOCKS[block]
        row = lax.broadcasted_iota(jnp.int32, (SUBLANES, slots), 0)
        for cell in range(cells):
            span = slice(cell * slots, (cell + 1) * slots)
            shift_y = CELL_SIDE * block_row(cell, half, cells)
            lift = jnp.where(row == 0, CELL_SIDE * x_offset, jnp.where(row == 1, shift_y, 0.0))
            src[block, :, span] = block_stat[:, span] + lift

    prepare(0, stat)
    for cell in range(cells):
        span = slice(cell * slots, (cell + 1) * slots)
        columns = jnp.transpose(stat[:, span])
        for at, (row, factor, shift) in enumerate(
            (
                (0, 1.0, 0.0),
                (1, 1.0, CELL_SIDE * cell),
                (2, 1.0, 0.0),
                (3, -THOLE_DAMP, 0.0),
                (7, 1.0, 0.0),
            )
        ):
            column = columns[:, row : row + 1] * factor + shift
            tgt[at, span, :] = jnp.broadcast_to(column, (slots, LANES))

    sub = lax.broadcasted_iota(jnp.int32, (SUBLANES, LANES), 0)
    lane = lax.broadcasted_iota(jnp.int32, (SUBLANES, LANES), 1)
    chunks = [slice(at * LANES, (at + 1) * LANES) for at in range(width // LANES)]

    def inner(rows, vector):
        parts = [r * v for r, v in zip(rows, vector)]
        while len(parts) > 1:
            parts = [sum(parts[at : at + 2]) for at in range(0, len(parts), 2)]
        return jnp.sum(parts[0], axis=1, keepdims=True)

    hist_rows = [res_hist[:, chunk] for chunk in chunks]
    past_gram = jnp.zeros((SUBLANES, LANES), jnp.float32)
    for k in range(SUBLANES - 1):
        column = inner(hist_rows, [rows[k : k + 1] for rows in hist_rows])
        past_gram = past_gram + jnp.where(lane == k, column, 0.0)

    tile_index = [
        {key[:3]: at for at, key in enumerate(sources(c, range(len(BLOCKS)), cells, tiles))}
        for c in range(cells)
    ]

    def share(mine, sent, landed, sems):
        sent[...] = mine

        def copy_to(step):
            return pltpu.make_async_remote_copy(
                src_ref=sent,
                dst_ref=landed.at[step - 1],
                send_sem=sems.at[0],
                recv_sem=sems.at[1],
                device_id=other(step),
                device_id_type=MESH,
            )

        def send(step, carry):
            copy_to(step).start()
            return carry

        def start():
            lax.fori_loop(1, total, send, 0)

        def finish():
            pltpu.make_async_copy(landed, landed, sems.at[1]).wait()
            return mine + jnp.sum(landed[...], axis=0)

        def sent_all():
            pltpu.make_async_copy(landed, landed, sems.at[0]).wait()

        return start, finish, sent_all

    start_past, finish_past, past_sent = share(past_gram, past_send, past_recv, past_sem)
    hist_copies = halo_copies(out_hist, hist_halo, hist_sem)

    def first_field(phase, first):
        for c in range(cells):
            met = sources(c, phase, cells, tiles)

            def group(step, carry, c=c, met=met):
                local = pl.ds(pl.multiple_of(step * ROWS, ROWS), ROWS)
                at_slot = pl.ds(pl.multiple_of(c * slots + step * ROWS, ROWS), ROWS)
                ax, ay, az, an = (tgt[m, at_slot, :] for m in range(4))
                if first:
                    sums = [jnp.zeros((ROWS, LANES), jnp.float32)] * 3
                else:
                    sums = [acc[c, m, local, :] for m in range(3)]
                for block, cell, tile, same in met:
                    span = slice(cell * slots + tile * LANES, cell * slots + (tile + 1) * LANES)
                    bx, by, bz, bn, vx, vy, vz, bm = (
                        src[block, m : m + 1, span] for m in range(8)
                    )
                    dx, dy, dz = bx - ax, by - ay, bz - az
                    s = dx * dx + dy * dy + dz * dz + SOFTENING
                    inv = lax.rsqrt(s)
                    inv2 = inv * inv
                    inv3 = inv2 * inv
                    minus_x = (s * s) * inv * (an * bn)
                    e = jnp.exp(minus_x)
                    t = jnp.maximum(CUTOFF_SQ - s, 0.0)
                    w = t * t * inv3
                    if same:
                        w = jnp.where(tgt[4, at_slot, :] != bm, w, 0.0)
                    rest = 1.0 - e
                    iso_v = w * rest
                    ten_v = w * inv2 * (rest + minus_x * e)
                    where = tile_index[c][(block, cell, tile)]
                    pair[0, c, where, local, :] = iso_v
                    pair[1, c, where, local, :] = ten_v
                    q = ten_v * (dx * (3.0 * vx) + dy * (3.0 * vy) + dz * (3.0 * vz))
                    sums = [
                        sums[0] + (dx * q - iso_v * vx),
                        sums[1] + (dy * q - iso_v * vy),
                        sums[2] + (dz * q - iso_v * vz),
                    ]
                for m in range(3):
                    acc[c, m, local, :] = sums[m]
                return carry

            lax.fori_loop(0, slots // ROWS, group, 0)

    def form_tensors():
        for c in range(cells):
            met = sources(c, range(len(BLOCKS)), cells, tiles)

            def group(step, carry, c=c, met=met):
                local = pl.ds(pl.multiple_of(step * ROWS, ROWS), ROWS)
                at_slot = pl.ds(pl.multiple_of(c * slots + step * ROWS, ROWS), ROWS)
                ax, ay, az = (tgt[m, at_slot, :] for m in range(3))
                for at, (block, cell, tile, _) in enumerate(met):
                    first = cell * slots + tile * LANES
                    bx, by, bz = (src[block, m : m + 1, first : first + LANES] for m in range(3))
                    dx, dy, dz = bx - ax, by - ay, bz - az
                    iso_v = pair[0, c, at, local, :]
                    ten_v = pair[1, c, at, local, :] * 3.0
                    tx, ty, tz = ten_v * dx, ten_v * dy, ten_v * dz
                    pair[0, c, at, local, :] = tx * dx - iso_v
                    pair[1, c, at, local, :] = tx * dy
                    pair[2, c, at, local, :] = tx * dz
                    pair[3, c, at, local, :] = ty * dy - iso_v
                    pair[4, c, at, local, :] = ty * dz
                    pair[5, c, at, local, :] = tz * dz - iso_v
                return carry

            lax.fori_loop(0, slots // ROWS, group, 0)

    def second_field():
        for c in range(cells):
            met = sources(c, range(len(BLOCKS)), cells, tiles)

            def group(step, carry, c=c, met=met):
                local = pl.ds(pl.multiple_of(step * ROWS, ROWS), ROWS)
                sums = [jnp.zeros((ROWS, LANES), jnp.float32)] * 3
                for at, (block, cell, tile, _) in enumerate(met):
                    starts = [(cell * 3 + m) * slots + tile * LANES for m in range(3)]
                    vx, vy, vz = (vec[block : block + 1, at : at + LANES] for at in starts)
                    xx, xy, xz, yy, yz, zz = (pair[n, c, at, local, :] for n in range(6))
                    sums = [
                        sums[0] + (xx * vx + xy * vy + xz * vz),
                        sums[1] + (xy * vx + yy * vy + yz * vz),
                        sums[2] + (xz * vx + yz * vy + zz * vz),
                    ]
                for m in range(3):
                    acc[c, m, local, :] = sums[m]
                return carry

            lax.fori_loop(0, slots // ROWS, group, 0)

    def jacobi_rows():
        found = []
        for c in range(cells):
            for m in range(3):
                for tile in range(tiles):
                    part = acc[c, m, tile * LANES : (tile + 1) * LANES, :]
                    field = jnp.sum(jnp.transpose(part), axis=0, keepdims=True)
                    span = slice(tile * LANES, (tile + 1) * LANES)
                    field = permanent[m, c : c + 1, span] + field * (1.0 / CUTOFF_SQ**2)
                    first = c * slots + tile * LANES
                    found.append(scale[0:1, first : first + LANES] * field)
        return found

    def as_row(column):
        return jnp.sum(jnp.where(sub == lane, column, 0.0), axis=0, keepdims=True)

    def mirrored(gram, row, k):
        column = jnp.sum(jnp.where(sub == lane, row, 0.0), axis=1, keepdims=True)
        return jnp.where(lane == k, column, jnp.where(sub == k, row, gram))

    def solve(gram):
        held = jnp.where(lane == SUBLANES, 1.0, gram)
        for k in range(SUBLANES):
            column = jnp.broadcast_to(held[:, k : k + 1], held.shape)
            pivot_row = held[k : k + 1, :] / column[k : k + 1, :]
            held = jnp.where(sub == k, pivot_row, held - column * pivot_row)
        y = jnp.broadcast_to(held[:, SUBLANES : SUBLANES + 1], held.shape)
        return y / jnp.sum(y, axis=0, keepdims=True)

    def mixed(hist, weights, chunk):
        return jnp.sum(weights * hist, axis=0, keepdims=True)

    newest = SUBLANES - 1
    for at, phase in enumerate(PHASES):
        for block in phase:
            if block:
                stat_copies[block - 1].wait_recv()
                prepare(block, stat_halo.at[block - 1])
        if at == len(PHASES) - 1:
            start_past()
            for copy in hist_copies:
                copy.start()
        first_field(phase, at == 0)

    jacobi = jacobi_rows()
    for row, chunk in zip(jacobi, chunks):
        jac_own[0:1, chunk] = row
    jac_copies = halo_copies(jac_own, jac_halo, jac_sem)
    residual = []
    for at, chunk in enumerate(chunks):
        cell, rest = divmod(at, 3 * tiles)
        m, tile = divmod(rest, tiles)
        first = cell * slots + tile * LANES
        residual.append(jacobi[at] - stat[4 + m : 5 + m, first : first + LANES])
    res_rows = [jnp.where(sub == newest, r, rows) for r, rows in zip(residual, hist_rows)]
    row = as_row(inner(res_rows, residual))
    start, finish, first_sent = share(row, row_send.at[0], row_recv.at[0], row_sem.at[0])
    for copy in jac_copies:
        copy.start()
    start()
    form_tensors()
    past_gram = finish_past()
    gram = mirrored(past_gram, finish(), newest)
    weights = solve(gram)

    current = []
    for at, chunk in enumerate(chunks):
        row = mixed(out_hist[:, chunk], weights, chunk) + weights[newest : newest + 1] * jacobi[at]
        current.append(row)
        vec[0:1, chunk] = row
    for block in range(1, len(BLOCKS)):
        hist_copies[block - 1].wait_recv()
        jac_copies[block - 1].wait_recv()
        for chunk in chunks:
            vec[block : block + 1, chunk] = (
                mixed(hist_halo[block - 1, :, chunk], weights, chunk)
                + weights[newest : newest + 1] * jac_halo[block - 1, 0:1, chunk]
            )
    second_field()

    jacobi_next = jacobi_rows()
    residual = [a - b for a, b in zip(jacobi_next, current)]
    res_rows = [jnp.where(sub == 0, r, rows) for r, rows in zip(residual, res_rows)]
    row = as_row(inner(res_rows, residual))
    start, finish, second_sent = share(row, row_send.at[1], row_recv.at[1], row_sem.at[1])
    start()
    gram = mirrored(gram, finish(), 0)
    weights = solve(gram)
    kept = jnp.where(sub == 0, 0.0, weights)
    for at, chunk in enumerate(chunks):
        cell, rest = divmod(at, 3 * tiles)
        m, tile = divmod(rest, tiles)
        next_ref[0, m, cell : cell + 1, tile * LANES : (tile + 1) * LANES] = (
            mixed(out_hist[:, chunk], kept, chunk)
            + weights[newest : newest + 1] * jac_own[0:1, chunk]
            + weights[0:1] * jacobi_next[at]
        )
    column = jnp.concatenate([weights[1:], weights[0:1]], axis=0)
    weight_ref[...] = as_row(column)[0, :SUBLANES]

    for copy in stat_copies + hist_copies + jac_copies:
        copy.wait_send()
    past_sent()
    first_sent()
    second_sent()


def wired(arg_count, nx, ny, cells, slots, tile_width, counts, *refs):
    args, rest = refs[:arg_count], refs[arg_count:]
    outs, rest = rest[:2], rest[2:]
    held, rest = rest[:arg_count], rest[arg_count:]
    kernel(nx, ny, cells, slots, tile_width, counts, args, outs, held, *rest)


def body(nx, ny, positions, polarizability, tile_counts, molecules, perm_field, dipoles, past_out, past_res):
    cells, tile_count = tile_counts.shape[1:]
    slots = positions.shape[-1]
    tile_width = slots // tile_count
    tiles = slots // LANES
    past = past_out.shape[2]
    assert ny == 2 and nx > 2 and cells > 1 and past + 1 == SUBLANES and slots % LANES == 0
    width = cells * 3 * slots

    halo = len(BLOCKS) - 1
    met = len(sources(0, range(len(BLOCKS)), cells, tiles))
    vmem = pl.BlockSpec(memory_space=pltpu.VMEM)
    hbm = pl.BlockSpec(memory_space=pltpu.HBM)
    raw = (
        jnp.swapaxes(positions, 1, 2),
        polarizability,
        molecules,
        jnp.swapaxes(perm_field, 1, 2),
        jnp.swapaxes(dipoles, 1, 2),
        jnp.transpose(past_out, (0, 2, 3, 1, 4)),
        jnp.transpose(past_res, (0, 2, 3, 1, 4)),
    )
    pairs_kept = cells * slots * met * LANES
    current, weights = pl.pallas_call(
        functools.partial(wired, len(raw), nx, ny, cells, slots, tile_width),
        out_shape=(
            jax.ShapeDtypeStruct((1, 3, cells, slots), jnp.float32),
            jax.ShapeDtypeStruct((SUBLANES,), jnp.float32),
        ),
        in_specs=[pl.BlockSpec(memory_space=pltpu.SMEM)] + [hbm] * len(raw),
        out_specs=(vmem, vmem),
        scratch_shapes=[pltpu.VMEM(arg.shape[1:], arg.dtype) for arg in raw]
        + [
            pltpu.VMEM((SUBLANES, cells * slots), jnp.float32),
            pltpu.VMEM((SUBLANES, width), jnp.float32),
            pltpu.VMEM((SUBLANES, width), jnp.float32),
            pltpu.VMEM((1, cells * slots), jnp.float32),
            pltpu.VMEM((halo, SUBLANES, cells * slots), jnp.float32),
            pltpu.VMEM((halo, SUBLANES, width), jnp.float32),
            pltpu.VMEM((halo, 1, width), jnp.float32),
            pltpu.VMEM((halo + 1, SUBLANES, cells * slots), jnp.float32),
            pltpu.VMEM((5, cells * slots, LANES), jnp.float32),
            pltpu.VMEM((6, cells, met, slots, LANES), jnp.float32),
            pltpu.VMEM((cells, 3, slots, LANES), jnp.float32),
            pltpu.VMEM((1, width), jnp.float32),
            pltpu.VMEM((SUBLANES, width), jnp.float32),
            pltpu.VMEM((SUBLANES, LANES), jnp.float32),
            pltpu.VMEM((nx * ny - 1, SUBLANES, LANES), jnp.float32),
            pltpu.VMEM((2, 1, LANES), jnp.float32),
            pltpu.VMEM((2, nx * ny - 1, 1, LANES), jnp.float32),
            pltpu.SemaphoreType.DMA((len(raw),)),
            pltpu.SemaphoreType.DMA((2, halo)),
            pltpu.SemaphoreType.DMA((2, halo)),
            pltpu.SemaphoreType.DMA((2, halo)),
            pltpu.SemaphoreType.DMA((2,)),
            pltpu.SemaphoreType.DMA((2, 2)),
        ],
        compiler_params=pltpu.CompilerParams(
            collective_id=0, has_side_effects=True, vmem_limit_bytes=56 * 1024 * 1024
        ),
        cost_estimate=pl.CostEstimate(
            flops=70 * pairs_kept, bytes_accessed=16 * width * SUBLANES, transcendentals=2 * pairs_kept
        ),
    )(tile_counts, *raw)
    return (jnp.swapaxes(current, 1, 2), weights)


def solution(mesh):
    cell_axes = P(("box", "gx"), "gy")
    return jax.shard_map(
        functools.partial(body, mesh.shape["gx"], mesh.shape["gy"]),
        mesh=mesh,
        in_specs=(cell_axes,) * 8,
        out_specs=(cell_axes, P("box")),
        check_vma=False,
    )
```

```python
import functools

import jax
import jax.numpy as jnp
from jax import lax
from jax.experimental import pallas as pl
from jax.experimental.pallas import tpu as pltpu
from jax.sharding import PartitionSpec as P

CELL_SIDE = 9.0
CUTOFF_SQ = 81.0
SOFTENING = 0.25
THOLE_DAMP = 0.39
LANES = 128
SUBLANES = 8
ROWS = 32
MESH = pl.DeviceIdType.MESH

BLOCKS = ((0, 0), (0, 1), (1, 0), (1, 1), (-1, 0), (-1, 1))
PHASES = ((0,), (1,), (2, 3), (4, 5))


def block_row(cell, half, cells):
    if half == 0:
        return cell
    return -1 if cell == cells - 1 else cells


def sources(target_cell, blocks, cells, tiles):
    found = []
    for block in blocks:
        x_offset, half = BLOCKS[block]
        for cell in range(cells):
            if half == 1 and cell not in (0, cells - 1):
                continue
            if abs(block_row(cell, half, cells) - target_cell) > 1:
                continue
            for tile in range(tiles):
                found.append((block, cell, tile, block == 0 and cell == target_cell))
    return found


def kernel(
    nx,
    ny,
    cells,
    slots,
    tile_width,
    args,
    outs,
    held,
    stat,
    out_hist,
    res_hist,
    scale,
    stat_halo,
    hist_halo,
    jac_halo,
    src,
    tgt,
    pair,
    acc,
    jac_own,
    vec,
    past_send,
    past_recv,
    row_send,
    row_recv,
    in_sem,
    stat_sem,
    hist_sem,
    jac_sem,
    past_sem,
    row_sem,
):
    next_ref, weight_ref = outs
    positions, polarity, molecules, permanent, dipoles, past_out, past_res, counts = held
    tiles = slots // LANES
    width = cells * 3 * slots
    total = nx * ny
    my_x = lax.axis_index("gx")
    my_y = lax.axis_index("gy")
    me = my_x * ny + my_y

    def other(step):
        flat = lax.rem(me + step, total)
        return {"gx": flat // ny, "gy": lax.rem(flat, ny)}

    barrier = pltpu.get_barrier_semaphore()

    def greet(step, carry):
        pl.semaphore_signal(barrier, inc=1, device_id=other(step), device_id_type=MESH)
        return carry

    lax.fori_loop(1, total, greet, 0)
    fetches = [
        pltpu.make_async_copy(arg.at[0], into, in_sem.at[at])
        for at, (arg, into) in enumerate(zip(args, held))
    ]
    for fetch in fetches:
        fetch.start()

    def halo_copies(source, landing, sems):
        copies = []
        for at, (x_offset, half) in enumerate(BLOCKS[1:]):
            target = {
                "gx": lax.rem(my_x - x_offset + nx, nx),
                "gy": lax.rem(my_y + half, ny),
            }
            copies.append(
                pltpu.make_async_remote_copy(
                    src_ref=source,
                    dst_ref=landing.at[at],
                    send_sem=sems.at[0, at],
                    recv_sem=sems.at[1, at],
                    device_id=target,
                    device_id_type=MESH,
                )
            )
        return copies

    index = lax.broadcasted_iota(jnp.int32, (1, slots), 1)
    for fetch in fetches:
        fetch.wait()
    occupied = []
    for cell in range(cells):
        live = jnp.zeros((1, slots), jnp.float32)
        for tile in range(slots // tile_width):
            first = tile * tile_width
            inside = jnp.logical_and(index >= first, index < first + counts[cell, tile])
            live = jnp.where(inside, 1.0, live)
        occupied.append(live)

    for cell in range(cells):
        span = slice(cell * slots, (cell + 1) * slots)
        polar = polarity[cell : cell + 1, :]
        for m in range(3):
            stat[m : m + 1, span] = positions[m, cell : cell + 1, :]
            stat[4 + m : 5 + m, span] = dipoles[m, cell : cell + 1, :] * occupied[cell]
        stat[3:4, span] = lax.rsqrt(polar)
        stat[7:8, span] = molecules[cell : cell + 1, :].astype(jnp.float32)
        scale[0:1, span] = polar * occupied[cell]
    pl.semaphore_wait(barrier, total - 1)
    stat_copies = halo_copies(stat, stat_halo, stat_sem)
    for copy in stat_copies:
        copy.start()

    for stored, hist in ((past_res, res_hist), (past_out, out_hist)):
        hist[SUBLANES - 1 :, :] = jnp.zeros((1, width), jnp.float32)
        for cell in range(cells):
            for m in range(3):
                first = (cell * 3 + m) * slots
                for k in range(SUBLANES - 1):
                    row = stored[k, m, cell : cell + 1, :] * occupied[cell]
                    hist[k : k + 1, first : first + slots] = row

    def prepare(block, block_stat):
        x_offset, half = BLOCKS[block]
        row = lax.broadcasted_iota(jnp.int32, (SUBLANES, slots), 0)
        for cell in range(cells):
            span = slice(cell * slots, (cell + 1) * slots)
            shift_y = CELL_SIDE * block_row(cell, half, cells)
            lift = jnp.where(row == 0, CELL_SIDE * x_offset, jnp.where(row == 1, shift_y, 0.0))
            src[block, :, span] = block_stat[:, span] + lift

    prepare(0, stat)
    for cell in range(cells):
        span = slice(cell * slots, (cell + 1) * slots)
        columns = jnp.transpose(stat[:, span])
        for at, (row, factor, shift) in enumerate(
            (
                (0, 1.0, 0.0),
                (1, 1.0, CELL_SIDE * cell),
                (2, 1.0, 0.0),
                (3, -THOLE_DAMP, 0.0),
                (7, 1.0, 0.0),
            )
        ):
            column = columns[:, row : row + 1] * factor + shift
            tgt[at, span, :] = jnp.broadcast_to(column, (slots, LANES))

    sub = lax.broadcasted_iota(jnp.int32, (SUBLANES, LANES), 0)
    lane = lax.broadcasted_iota(jnp.int32, (SUBLANES, LANES), 1)
    chunks = [slice(at * LANES, (at + 1) * LANES) for at in range(width // LANES)]

    def inner(rows, vector):
        parts = [r * v for r, v in zip(rows, vector)]
        while len(parts) > 1:
            parts = [sum(parts[at : at + 2]) for at in range(0, len(parts), 2)]
        return jnp.sum(parts[0], axis=1, keepdims=True)

    hist_rows = [res_hist[:, chunk] for chunk in chunks]
    past_gram = jnp.zeros((SUBLANES, LANES), jnp.float32)
    for k in range(SUBLANES - 1):
        column = inner(hist_rows, [rows[k : k + 1] for rows in hist_rows])
        past_gram = past_gram + jnp.where(lane == k, column, 0.0)

    tile_index = [
        {key[:3]: at for at, key in enumerate(sources(c, range(len(BLOCKS)), cells, tiles))}
        for c in range(cells)
    ]

    def share(mine, sent, landed, sems):
        sent[...] = mine

        def copy_to(step):
            return pltpu.make_async_remote_copy(
                src_ref=sent,
                dst_ref=landed.at[step - 1],
                send_sem=sems.at[0],
                recv_sem=sems.at[1],
                device_id=other(step),
                device_id_type=MESH,
            )

        def send(step, carry):
            copy_to(step).start()
            return carry

        def start():
            lax.fori_loop(1, total, send, 0)

        def finish():
            pltpu.make_async_copy(landed, landed, sems.at[1]).wait()
            return mine + jnp.sum(landed[...], axis=0)

        def sent_all():
            pltpu.make_async_copy(landed, landed, sems.at[0]).wait()

        return start, finish, sent_all

    start_past, finish_past, past_sent = share(past_gram, past_send, past_recv, past_sem)
    hist_copies = halo_copies(out_hist, hist_halo, hist_sem)

    def first_field(phase, first):
        for c in range(cells):
            met = sources(c, phase, cells, tiles)

            def group(step, carry, c=c, met=met):
                local = pl.ds(pl.multiple_of(step * ROWS, ROWS), ROWS)
                at_slot = pl.ds(pl.multiple_of(c * slots + step * ROWS, ROWS), ROWS)
                ax, ay, az, an = (tgt[m, at_slot, :] for m in range(4))
                if first:
                    sums = [jnp.zeros((ROWS, LANES), jnp.float32)] * 3
                else:
                    sums = [acc[c, m, local, :] for m in range(3)]
                for block, cell, tile, same in met:
                    span = slice(cell * slots + tile * LANES, cell * slots + (tile + 1) * LANES)
                    bx, by, bz, bn, vx, vy, vz, bm = (
                        src[block, m : m + 1, span] for m in range(8)
                    )
                    dx, dy, dz = bx - ax, by - ay, bz - az
                    s = dx * dx + dy * dy + dz * dz + SOFTENING
                    inv = lax.rsqrt(s)
                    inv2 = inv * inv
                    inv3 = inv2 * inv
                    minus_x = (s * s) * inv * (an * bn)
                    e = jnp.exp(minus_x)
                    t = jnp.maximum(CUTOFF_SQ - s, 0.0)
                    w = t * t * inv3
                    if same:
                        w = jnp.where(tgt[4, at_slot, :] != bm, w, 0.0)
                    rest = 1.0 - e
                    iso_v = w * rest
                    ten_v = w * inv2 * (rest + minus_x * e)
                    where = tile_index[c][(block, cell, tile)]
                    pair[0, c, where, local, :] = iso_v
                    pair[1, c, where, local, :] = ten_v
                    q = ten_v * (dx * (3.0 * vx) + dy * (3.0 * vy) + dz * (3.0 * vz))
                    sums = [
                        sums[0] + (dx * q - iso_v * vx),
                        sums[1] + (dy * q - iso_v * vy),
                        sums[2] + (dz * q - iso_v * vz),
                    ]
                for m in range(3):
                    acc[c, m, local, :] = sums[m]
                return carry

            lax.fori_loop(0, slots // ROWS, group, 0)

    def second_field():
        for c in range(cells):
            met = sources(c, range(len(BLOCKS)), cells, tiles)

            def group(step, carry, c=c, met=met):
                local = pl.ds(pl.multiple_of(step * ROWS, ROWS), ROWS)
                at_slot = pl.ds(pl.multiple_of(c * slots + step * ROWS, ROWS), ROWS)
                ax, ay, az = (tgt[m, at_slot, :] for m in range(3))
                sums = [jnp.zeros((ROWS, LANES), jnp.float32)] * 3
                for block, cell, tile, _ in met:
                    first = cell * slots + tile * LANES
                    bx, by, bz = (src[block, m : m + 1, first : first + LANES] for m in range(3))
                    starts = [(cell * 3 + m) * slots + tile * LANES for m in range(3)]
                    vx, vy, vz = (vec[block : block + 1, at : at + LANES] for at in starts)
                    dx, dy, dz = bx - ax, by - ay, bz - az
                    where = tile_index[c][(block, cell, tile)]
                    iso_v = pair[0, c, where, local, :]
                    q = pair[1, c, where, local, :] * (dx * (3.0 * vx) + dy * (3.0 * vy) + dz * (3.0 * vz))
                    sums = [
                        sums[0] + (dx * q - iso_v * vx),
                        sums[1] + (dy * q - iso_v * vy),
                        sums[2] + (dz * q - iso_v * vz),
                    ]
                for m in range(3):
                    acc[c, m, local, :] = sums[m]
                return carry

            lax.fori_loop(0, slots // ROWS, group, 0)

    def jacobi_rows():
        found = []
        for c in range(cells):
            for m in range(3):
                for tile in range(tiles):
                    part = acc[c, m, tile * LANES : (tile + 1) * LANES, :]
                    field = jnp.sum(jnp.transpose(part), axis=0, keepdims=True)
                    span = slice(tile * LANES, (tile + 1) * LANES)
                    field = permanent[m, c : c + 1, span] + field * (1.0 / CUTOFF_SQ**2)
                    first = c * slots + tile * LANES
                    found.append(scale[0:1, first : first + LANES] * field)
        return found

    def as_row(column):
        return jnp.sum(jnp.where(sub == lane, column, 0.0), axis=0, keepdims=True)

    def mirrored(gram, row, k):
        column = jnp.sum(jnp.where(sub == lane, row, 0.0), axis=1, keepdims=True)
        return jnp.where(lane == k, column, jnp.where(sub == k, row, gram))

    def solve(gram):
        held = jnp.where(lane == SUBLANES, 1.0, gram)
        for k in range(SUBLANES):
            column = jnp.broadcast_to(held[:, k : k + 1], held.shape)
            pivot_row = held[k : k + 1, :] / column[k : k + 1, :]
            held = jnp.where(sub == k, pivot_row, held - column * pivot_row)
        y = jnp.broadcast_to(held[:, SUBLANES : SUBLANES + 1], held.shape)
        return y / jnp.sum(y, axis=0, keepdims=True)

    def mixed(hist, weights, chunk):
        return jnp.sum(weights * hist, axis=0, keepdims=True)

    newest = SUBLANES - 1
    for at, phase in enumerate(PHASES):
        for block in phase:
            if block:
                stat_copies[block - 1].wait_recv()
                prepare(block, stat_halo.at[block - 1])
        if at == len(PHASES) - 1:
            start_past()
            for copy in hist_copies:
                copy.start()
        first_field(phase, at == 0)

    jacobi = jacobi_rows()
    for row, chunk in zip(jacobi, chunks):
        jac_own[0:1, chunk] = row
    jac_copies = halo_copies(jac_own, jac_halo, jac_sem)
    residual = []
    for at, chunk in enumerate(chunks):
        cell, rest = divmod(at, 3 * tiles)
        m, tile = divmod(rest, tiles)
        first = cell * slots + tile * LANES
        residual.append(jacobi[at] - stat[4 + m : 5 + m, first : first + LANES])
    res_rows = [jnp.where(sub == newest, r, rows) for r, rows in zip(residual, hist_rows)]
    row = as_row(inner(res_rows, residual))
    start, finish, first_sent = share(row, row_send.at[0], row_recv.at[0], row_sem.at[0])
    for copy in jac_copies:
        copy.start()
    start()
    past_gram = finish_past()
    gram = mirrored(past_gram, finish(), newest)
    weights = solve(gram)

    current = []
    for at, chunk in enumerate(chunks):
        row = mixed(out_hist[:, chunk], weights, chunk) + weights[newest : newest + 1] * jacobi[at]
        current.append(row)
        vec[0:1, chunk] = row
    for block in range(1, len(BLOCKS)):
        hist_copies[block - 1].wait_recv()
        jac_copies[block - 1].wait_recv()
        for chunk in chunks:
            vec[block : block + 1, chunk] = (
                mixed(hist_halo[block - 1, :, chunk], weights, chunk)
                + weights[newest : newest + 1] * jac_halo[block - 1, 0:1, chunk]
            )
    second_field()

    jacobi_next = jacobi_rows()
    residual = [a - b for a, b in zip(jacobi_next, current)]
    res_rows = [jnp.where(sub == 0, r, rows) for r, rows in zip(residual, res_rows)]
    row = as_row(inner(res_rows, residual))
    start, finish, second_sent = share(row, row_send.at[1], row_recv.at[1], row_sem.at[1])
    start()
    gram = mirrored(gram, finish(), 0)
    weights = solve(gram)
    kept = jnp.where(sub == 0, 0.0, weights)
    for at, chunk in enumerate(chunks):
        cell, rest = divmod(at, 3 * tiles)
        m, tile = divmod(rest, tiles)
        next_ref[0, m, cell : cell + 1, tile * LANES : (tile + 1) * LANES] = (
            mixed(out_hist[:, chunk], kept, chunk)
            + weights[newest : newest + 1] * jac_own[0:1, chunk]
            + weights[0:1] * jacobi_next[at]
        )
    column = jnp.concatenate([weights[1:], weights[0:1]], axis=0)
    weight_ref[...] = as_row(column)[0, :SUBLANES]

    for copy in stat_copies + hist_copies + jac_copies:
        copy.wait_send()
    past_sent()
    first_sent()
    second_sent()


def wired(arg_count, nx, ny, cells, slots, tile_width, counts_arg, *refs):
    args, rest = refs[:arg_count], refs[arg_count:]
    outs, rest = rest[:2], rest[2:]
    held, rest = rest[:arg_count], rest[arg_count:]
    counts, *rest = rest
    args, inside = (*args, counts_arg), (*held, counts)
    kernel(nx, ny, cells, slots, tile_width, args, outs, inside, *rest)


def body(nx, ny, positions, polarizability, tile_counts, molecules, perm_field, dipoles, past_out, past_res):
    cells, tile_count = tile_counts.shape[1:]
    slots = positions.shape[-1]
    tile_width = slots // tile_count
    tiles = slots // LANES
    past = past_out.shape[2]
    assert ny == 2 and nx > 2 and cells > 1 and past + 1 == SUBLANES and slots % LANES == 0
    width = cells * 3 * slots

    halo = len(BLOCKS) - 1
    met = len(sources(0, range(len(BLOCKS)), cells, tiles))
    vmem = pl.BlockSpec(memory_space=pltpu.VMEM)
    hbm = pl.BlockSpec(memory_space=pltpu.HBM)
    raw = (
        jnp.swapaxes(positions, 1, 2),
        polarizability,
        molecules,
        jnp.swapaxes(perm_field, 1, 2),
        jnp.swapaxes(dipoles, 1, 2),
        jnp.transpose(past_out, (0, 2, 3, 1, 4)),
        jnp.transpose(past_res, (0, 2, 3, 1, 4)),
    )
    tile_counts, *raw = (
        pltpu.with_memory_space_constraint(arg, pltpu.HBM) for arg in (tile_counts, *raw)
    )
    pairs_kept = cells * slots * met * LANES
    current, weights = pl.pallas_call(
        functools.partial(wired, len(raw), nx, ny, cells, slots, tile_width),
        out_shape=(
            jax.ShapeDtypeStruct((1, 3, cells, slots), jnp.float32),
            jax.ShapeDtypeStruct((SUBLANES,), jnp.float32),
        ),
        in_specs=[hbm] * (1 + len(raw)),
        out_specs=(vmem, vmem),
        scratch_shapes=[pltpu.VMEM(arg.shape[1:], arg.dtype) for arg in raw]
        + [
            pltpu.SMEM(tile_counts.shape[1:], tile_counts.dtype),
            pltpu.VMEM((SUBLANES, cells * slots), jnp.float32),
            pltpu.VMEM((SUBLANES, width), jnp.float32),
            pltpu.VMEM((SUBLANES, width), jnp.float32),
            pltpu.VMEM((1, cells * slots), jnp.float32),
            pltpu.VMEM((halo, SUBLANES, cells * slots), jnp.float32),
            pltpu.VMEM((halo, SUBLANES, width), jnp.float32),
            pltpu.VMEM((halo, 1, width), jnp.float32),
            pltpu.VMEM((halo + 1, SUBLANES, cells * slots), jnp.float32),
            pltpu.VMEM((5, cells * slots, LANES), jnp.float32),
            pltpu.VMEM((2, cells, met, slots, LANES), jnp.float32),
            pltpu.VMEM((cells, 3, slots, LANES), jnp.float32),
            pltpu.VMEM((1, width), jnp.float32),
            pltpu.VMEM((SUBLANES, width), jnp.float32),
            pltpu.VMEM((SUBLANES, LANES), jnp.float32),
            pltpu.VMEM((nx * ny - 1, SUBLANES, LANES), jnp.float32),
            pltpu.VMEM((2, 1, LANES), jnp.float32),
            pltpu.VMEM((2, nx * ny - 1, 1, LANES), jnp.float32),
            pltpu.SemaphoreType.DMA((len(raw) + 1,)),
            pltpu.SemaphoreType.DMA((2, halo)),
            pltpu.SemaphoreType.DMA((2, halo)),
            pltpu.SemaphoreType.DMA((2, halo)),
            pltpu.SemaphoreType.DMA((2,)),
            pltpu.SemaphoreType.DMA((2, 2)),
        ],
        compiler_params=pltpu.CompilerParams(
            collective_id=0, has_side_effects=True, vmem_limit_bytes=24 * 1024 * 1024
        ),
        cost_estimate=pl.CostEstimate(
            flops=70 * pairs_kept, bytes_accessed=16 * width * SUBLANES, transcendentals=2 * pairs_kept
        ),
    )(tile_counts, *raw)
    return (jnp.swapaxes(current, 1, 2), weights)


def solution(mesh):
    cell_axes = P(("box", "gx"), "gy")
    return jax.shard_map(
        functools.partial(body, mesh.shape["gx"], mesh.shape["gy"]),
        mesh=mesh,
        in_specs=(cell_axes,) * 8,
        out_specs=(cell_axes, P("box")),
        check_vma=False,
    )
```

```python
import functools

import jax
import jax.numpy as jnp
from jax import lax
from jax.experimental import pallas as pl
from jax.experimental.pallas import tpu as pltpu
from jax.sharding import PartitionSpec as P

CELL_SIDE = 9.0
CUTOFF_SQ = 81.0
SOFTENING = 0.25
THOLE_DAMP = 0.39
LANES = 128
SUBLANES = 8
ROWS = 32
MESH = pl.DeviceIdType.MESH

BLOCKS = ((0, 0), (0, 1), (1, 0), (1, 1), (-1, 0), (-1, 1))
PHASES = ((0,), (1,), (2, 3), (4, 5))


def block_row(cell, half, cells):
    if half == 0:
        return cell
    return -1 if cell == cells - 1 else cells


def sources(target_cell, blocks, cells, tiles):
    found = []
    for block in blocks:
        x_offset, half = BLOCKS[block]
        for cell in range(cells):
            if half == 1 and cell not in (0, cells - 1):
                continue
            if abs(block_row(cell, half, cells) - target_cell) > 1:
                continue
            for tile in range(tiles):
                found.append((block, cell, tile, block == 0 and cell == target_cell))
    return found


def kernel(
    nx,
    ny,
    cells,
    slots,
    tile_width,
    args,
    outs,
    held,
    stat,
    out_hist,
    res_hist,
    scale,
    stat_halo,
    hist_halo,
    jac_halo,
    src,
    tgt,
    pair,
    acc,
    jac_own,
    vec,
    past_send,
    past_recv,
    row_send,
    row_recv,
    in_sem,
    stat_sem,
    hist_sem,
    jac_sem,
    past_sem,
    row_sem,
):
    next_ref, weight_ref = outs
    positions, polarity, molecules, permanent, dipoles, past_out, past_res, counts = held
    tiles = slots // LANES
    width = cells * 3 * slots
    total = nx * ny
    my_x = lax.axis_index("gx")
    my_y = lax.axis_index("gy")
    me = my_x * ny + my_y

    def other(step):
        flat = lax.rem(me + step, total)
        return {"gx": flat // ny, "gy": lax.rem(flat, ny)}

    barrier = pltpu.get_barrier_semaphore()

    def greet(step, carry):
        pl.semaphore_signal(barrier, inc=1, device_id=other(step), device_id_type=MESH)
        return carry

    lax.fori_loop(1, total, greet, 0)
    fetches = [
        pltpu.make_async_copy(arg.at[0], into, in_sem.at[at])
        for at, (arg, into) in enumerate(zip(args, held))
    ]
    for fetch in fetches:
        fetch.start()

    def halo_copies(source, landing, sems):
        copies = []
        for at, (x_offset, half) in enumerate(BLOCKS[1:]):
            target = {
                "gx": lax.rem(my_x - x_offset + nx, nx),
                "gy": lax.rem(my_y + half, ny),
            }
            copies.append(
                pltpu.make_async_remote_copy(
                    src_ref=source,
                    dst_ref=landing.at[at],
                    send_sem=sems.at[0, at],
                    recv_sem=sems.at[1, at],
                    device_id=target,
                    device_id_type=MESH,
                )
            )
        return copies

    index = lax.broadcasted_iota(jnp.int32, (1, slots), 1)
    for fetch in fetches:
        fetch.wait()
    occupied = []
    for cell in range(cells):
        live = jnp.zeros((1, slots), jnp.float32)
        for tile in range(slots // tile_width):
            first = tile * tile_width
            inside = jnp.logical_and(index >= first, index < first + counts[cell, tile])
            live = jnp.where(inside, 1.0, live)
        occupied.append(live)

    for cell in range(cells):
        span = slice(cell * slots, (cell + 1) * slots)
        polar = polarity[cell : cell + 1, :]
        for m in range(3):
            stat[m : m + 1, span] = positions[m, cell : cell + 1, :]
            stat[4 + m : 5 + m, span] = dipoles[m, cell : cell + 1, :] * occupied[cell]
        stat[3:4, span] = lax.rsqrt(polar)
        stat[7:8, span] = molecules[cell : cell + 1, :].astype(jnp.float32)
        scale[0:1, span] = polar * occupied[cell]

    for stored, hist in ((past_res, res_hist), (past_out, out_hist)):
        hist[SUBLANES - 1 :, :] = jnp.zeros((1, width), jnp.float32)
        for cell in range(cells):
            for m in range(3):
                first = (cell * 3 + m) * slots
                for k in range(SUBLANES - 1):
                    row = stored[k, m, cell : cell + 1, :] * occupied[cell]
                    hist[k : k + 1, first : first + slots] = row

    def prepare(block, block_stat):
        x_offset, half = BLOCKS[block]
        row = lax.broadcasted_iota(jnp.int32, (SUBLANES, slots), 0)
        for cell in range(cells):
            span = slice(cell * slots, (cell + 1) * slots)
            shift_y = CELL_SIDE * block_row(cell, half, cells)
            lift = jnp.where(row == 0, CELL_SIDE * x_offset, jnp.where(row == 1, shift_y, 0.0))
            src[block, :, span] = block_stat[:, span] + lift

    prepare(0, stat)
    for cell in range(cells):
        span = slice(cell * slots, (cell + 1) * slots)
        columns = jnp.transpose(stat[:, span])
        for at, (row, factor, shift) in enumerate(
            (
                (0, 1.0, 0.0),
                (1, 1.0, CELL_SIDE * cell),
                (2, 1.0, 0.0),
                (3, -THOLE_DAMP, 0.0),
                (7, 1.0, 0.0),
            )
        ):
            column = columns[:, row : row + 1] * factor + shift
            tgt[at, span, :] = jnp.broadcast_to(column, (slots, LANES))

    sub = lax.broadcasted_iota(jnp.int32, (SUBLANES, LANES), 0)
    lane = lax.broadcasted_iota(jnp.int32, (SUBLANES, LANES), 1)
    chunks = [slice(at * LANES, (at + 1) * LANES) for at in range(width // LANES)]

    def inner(rows, vector):
        parts = [r * v for r, v in zip(rows, vector)]
        while len(parts) > 1:
            parts = [sum(parts[at : at + 2]) for at in range(0, len(parts), 2)]
        return jnp.sum(parts[0], axis=1, keepdims=True)

    hist_rows = [res_hist[:, chunk] for chunk in chunks]
    past_gram = jnp.zeros((SUBLANES, LANES), jnp.float32)
    for k in range(SUBLANES - 1):
        column = inner(hist_rows, [rows[k : k + 1] for rows in hist_rows])
        past_gram = past_gram + jnp.where(lane == k, column, 0.0)

    tile_index = [
        {key[:3]: at for at, key in enumerate(sources(c, range(len(BLOCKS)), cells, tiles))}
        for c in range(cells)
    ]

    def share(mine, sent, landed, sems):
        sent[...] = mine

        def copy_to(step):
            return pltpu.make_async_remote_copy(
                src_ref=sent,
                dst_ref=landed.at[step - 1],
                send_sem=sems.at[0],
                recv_sem=sems.at[1],
                device_id=other(step),
                device_id_type=MESH,
            )

        def send(step, carry):
            copy_to(step).start()
            return carry

        def start():
            lax.fori_loop(1, total, send, 0)

        def finish():
            pltpu.make_async_copy(landed, landed, sems.at[1]).wait()
            return mine + jnp.sum(landed[...], axis=0)

        def sent_all():
            pltpu.make_async_copy(landed, landed, sems.at[0]).wait()

        return start, finish, sent_all

    start_past, finish_past, past_sent = share(past_gram, past_send, past_recv, past_sem)
    hist_copies = halo_copies(out_hist, hist_halo, hist_sem)

    def first_field(phase, first):
        for c in range(cells):
            met = sources(c, phase, cells, tiles)

            def group(step, carry, c=c, met=met):
                local = pl.ds(pl.multiple_of(step * ROWS, ROWS), ROWS)
                at_slot = pl.ds(pl.multiple_of(c * slots + step * ROWS, ROWS), ROWS)
                ax, ay, az, an = (tgt[m, at_slot, :] for m in range(4))
                if first:
                    sums = [jnp.zeros((ROWS, LANES), jnp.float32)] * 3
                else:
                    sums = [acc[c, m, local, :] for m in range(3)]
                for block, cell, tile, same in met:
                    span = slice(cell * slots + tile * LANES, cell * slots + (tile + 1) * LANES)
                    bx, by, bz, bn, vx, vy, vz, bm = (
                        src[block, m : m + 1, span] for m in range(8)
                    )
                    dx, dy, dz = bx - ax, by - ay, bz - az
                    s = dx * dx + dy * dy + dz * dz + SOFTENING
                    inv = lax.rsqrt(s)
                    inv2 = inv * inv
                    inv3 = inv2 * inv
                    minus_x = (s * s) * inv * (an * bn)
                    e = jnp.exp(minus_x)
                    t = jnp.maximum(CUTOFF_SQ - s, 0.0)
                    w = t * t * inv3
                    if same:
                        w = jnp.where(tgt[4, at_slot, :] != bm, w, 0.0)
                    rest = 1.0 - e
                    iso_v = w * rest
                    ten_v = w * inv2 * (rest + minus_x * e)
                    where = tile_index[c][(block, cell, tile)]
                    pair[0, c, where, local, :] = iso_v
                    pair[1, c, where, local, :] = ten_v
                    q = ten_v * (dx * (3.0 * vx) + dy * (3.0 * vy) + dz * (3.0 * vz))
                    sums = [
                        sums[0] + (dx * q - iso_v * vx),
                        sums[1] + (dy * q - iso_v * vy),
                        sums[2] + (dz * q - iso_v * vz),
                    ]
                for m in range(3):
                    acc[c, m, local, :] = sums[m]
                return carry

            lax.fori_loop(0, slots // ROWS, group, 0)

    def second_field():
        for c in range(cells):
            met = sources(c, range(len(BLOCKS)), cells, tiles)

            def group(step, carry, c=c, met=met):
                local = pl.ds(pl.multiple_of(step * ROWS, ROWS), ROWS)
                at_slot = pl.ds(pl.multiple_of(c * slots + step * ROWS, ROWS), ROWS)
                ax, ay, az = (tgt[m, at_slot, :] for m in range(3))
                sums = [jnp.zeros((ROWS, LANES), jnp.float32)] * 3
                for block, cell, tile, _ in met:
                    first = cell * slots + tile * LANES
                    bx, by, bz = (src[block, m : m + 1, first : first + LANES] for m in range(3))
                    starts = [(cell * 3 + m) * slots + tile * LANES for m in range(3)]
                    vx, vy, vz = (vec[block : block + 1, at : at + LANES] for at in starts)
                    dx, dy, dz = bx - ax, by - ay, bz - az
                    where = tile_index[c][(block, cell, tile)]
                    iso_v = pair[0, c, where, local, :]
                    q = pair[1, c, where, local, :] * (dx * (3.0 * vx) + dy * (3.0 * vy) + dz * (3.0 * vz))
                    sums = [
                        sums[0] + (dx * q - iso_v * vx),
                        sums[1] + (dy * q - iso_v * vy),
                        sums[2] + (dz * q - iso_v * vz),
                    ]
                for m in range(3):
                    acc[c, m, local, :] = sums[m]
                return carry

            lax.fori_loop(0, slots // ROWS, group, 0)

    def jacobi_rows():
        found = []
        for c in range(cells):
            for m in range(3):
                for tile in range(tiles):
                    part = acc[c, m, tile * LANES : (tile + 1) * LANES, :]
                    field = jnp.sum(jnp.transpose(part), axis=0, keepdims=True)
                    span = slice(tile * LANES, (tile + 1) * LANES)
                    field = permanent[m, c : c + 1, span] + field * (1.0 / CUTOFF_SQ**2)
                    first = c * slots + tile * LANES
                    found.append(scale[0:1, first : first + LANES] * field)
        return found

    def as_row(column):
        return jnp.sum(jnp.where(sub == lane, column, 0.0), axis=0, keepdims=True)

    def mirrored(gram, row, k):
        column = jnp.sum(jnp.where(sub == lane, row, 0.0), axis=1, keepdims=True)
        return jnp.where(lane == k, column, jnp.where(sub == k, row, gram))

    def solve(gram):
        held = jnp.where(lane == SUBLANES, 1.0, gram)
        for k in range(SUBLANES):
            column = jnp.broadcast_to(held[:, k : k + 1], held.shape)
            pivot_row = held[k : k + 1, :] / column[k : k + 1, :]
            held = jnp.where(sub == k, pivot_row, held - column * pivot_row)
        y = jnp.broadcast_to(held[:, SUBLANES : SUBLANES + 1], held.shape)
        return y / jnp.sum(y, axis=0, keepdims=True)

    def mixed(hist, weights, chunk):
        return jnp.sum(weights * hist, axis=0, keepdims=True)

    newest = SUBLANES - 1
    pl.semaphore_wait(barrier, total - 1)
    stat_copies = halo_copies(stat, stat_halo, stat_sem)
    for copy in stat_copies:
        copy.start()

    for at, phase in enumerate(PHASES):
        for block in phase:
            if block:
                stat_copies[block - 1].wait_recv()
                prepare(block, stat_halo.at[block - 1])
        if at == len(PHASES) - 1:
            start_past()
            for copy in hist_copies:
                copy.start()
        first_field(phase, at == 0)

    jacobi = jacobi_rows()
    for row, chunk in zip(jacobi, chunks):
        jac_own[0:1, chunk] = row
    jac_copies = halo_copies(jac_own, jac_halo, jac_sem)
    residual = []
    for at, chunk in enumerate(chunks):
        cell, rest = divmod(at, 3 * tiles)
        m, tile = divmod(rest, tiles)
        first = cell * slots + tile * LANES
        residual.append(jacobi[at] - stat[4 + m : 5 + m, first : first + LANES])
    res_rows = [jnp.where(sub == newest, r, rows) for r, rows in zip(residual, hist_rows)]
    row = as_row(inner(res_rows, residual))
    start, finish, first_sent = share(row, row_send.at[0], row_recv.at[0], row_sem.at[0])
    for copy in jac_copies:
        copy.start()
    start()
    past_gram = finish_past()
    gram = mirrored(past_gram, finish(), newest)
    weights = solve(gram)

    current = []
    for at, chunk in enumerate(chunks):
        row = mixed(out_hist[:, chunk], weights, chunk) + weights[newest : newest + 1] * jacobi[at]
        current.append(row)
        vec[0:1, chunk] = row
    for block in range(1, len(BLOCKS)):
        hist_copies[block - 1].wait_recv()
        jac_copies[block - 1].wait_recv()
        for chunk in chunks:
            vec[block : block + 1, chunk] = (
                mixed(hist_halo[block - 1, :, chunk], weights, chunk)
                + weights[newest : newest + 1] * jac_halo[block - 1, 0:1, chunk]
            )
    second_field()

    jacobi_next = jacobi_rows()
    residual = [a - b for a, b in zip(jacobi_next, current)]
    res_rows = [jnp.where(sub == 0, r, rows) for r, rows in zip(residual, res_rows)]
    row = as_row(inner(res_rows, residual))
    start, finish, second_sent = share(row, row_send.at[1], row_recv.at[1], row_sem.at[1])
    start()
    gram = mirrored(gram, finish(), 0)
    weights = solve(gram)
    kept = jnp.where(sub == 0, 0.0, weights)
    for at, chunk in enumerate(chunks):
        cell, rest = divmod(at, 3 * tiles)
        m, tile = divmod(rest, tiles)
        next_ref[0, m, cell : cell + 1, tile * LANES : (tile + 1) * LANES] = (
            mixed(out_hist[:, chunk], kept, chunk)
            + weights[newest : newest + 1] * jac_own[0:1, chunk]
            + weights[0:1] * jacobi_next[at]
        )
    column = jnp.concatenate([weights[1:], weights[0:1]], axis=0)
    weight_ref[...] = as_row(column)[0, :SUBLANES]

    for copy in stat_copies + hist_copies + jac_copies:
        copy.wait_send()
    past_sent()
    first_sent()
    second_sent()


def wired(arg_count, nx, ny, cells, slots, tile_width, counts_arg, *refs):
    args, rest = refs[:arg_count], refs[arg_count:]
    outs, rest = rest[:2], rest[2:]
    held, rest = rest[:arg_count], rest[arg_count:]
    counts, *rest = rest
    args, inside = (*args, counts_arg), (*held, counts)
    kernel(nx, ny, cells, slots, tile_width, args, outs, inside, *rest)


def body(nx, ny, positions, polarizability, tile_counts, molecules, perm_field, dipoles, past_out, past_res):
    cells, tile_count = tile_counts.shape[1:]
    slots = positions.shape[-1]
    tile_width = slots // tile_count
    tiles = slots // LANES
    past = past_out.shape[2]
    assert ny == 2 and nx > 2 and cells > 1 and past + 1 == SUBLANES and slots % LANES == 0
    width = cells * 3 * slots

    halo = len(BLOCKS) - 1
    met = len(sources(0, range(len(BLOCKS)), cells, tiles))
    vmem = pl.BlockSpec(memory_space=pltpu.VMEM)
    hbm = pl.BlockSpec(memory_space=pltpu.HBM)
    raw = (
        jnp.swapaxes(positions, 1, 2),
        polarizability,
        molecules,
        jnp.swapaxes(perm_field, 1, 2),
        jnp.swapaxes(dipoles, 1, 2),
        jnp.transpose(past_out, (0, 2, 3, 1, 4)),
        jnp.transpose(past_res, (0, 2, 3, 1, 4)),
    )
    tile_counts, *raw = (
        pltpu.with_memory_space_constraint(arg, pltpu.HBM) for arg in (tile_counts, *raw)
    )
    pairs_kept = cells * slots * met * LANES
    current, weights = pl.pallas_call(
        functools.partial(wired, len(raw), nx, ny, cells, slots, tile_width),
        out_shape=(
            jax.ShapeDtypeStruct((1, 3, cells, slots), jnp.float32),
            jax.ShapeDtypeStruct((SUBLANES,), jnp.float32),
        ),
        in_specs=[hbm] * (1 + len(raw)),
        out_specs=(vmem, vmem),
        scratch_shapes=[pltpu.VMEM(arg.shape[1:], arg.dtype) for arg in raw]
        + [
            pltpu.SMEM(tile_counts.shape[1:], tile_counts.dtype),
            pltpu.VMEM((SUBLANES, cells * slots), jnp.float32),
            pltpu.VMEM((SUBLANES, width), jnp.float32),
            pltpu.VMEM((SUBLANES, width), jnp.float32),
            pltpu.VMEM((1, cells * slots), jnp.float32),
            pltpu.VMEM((halo, SUBLANES, cells * slots), jnp.float32),
            pltpu.VMEM((halo, SUBLANES, width), jnp.float32),
            pltpu.VMEM((halo, 1, width), jnp.float32),
            pltpu.VMEM((halo + 1, SUBLANES, cells * slots), jnp.float32),
            pltpu.VMEM((5, cells * slots, LANES), jnp.float32),
            pltpu.VMEM((2, cells, met, slots, LANES), jnp.float32),
            pltpu.VMEM((cells, 3, slots, LANES), jnp.float32),
            pltpu.VMEM((1, width), jnp.float32),
            pltpu.VMEM((SUBLANES, width), jnp.float32),
            pltpu.VMEM((SUBLANES, LANES), jnp.float32),
            pltpu.VMEM((nx * ny - 1, SUBLANES, LANES), jnp.float32),
            pltpu.VMEM((2, 1, LANES), jnp.float32),
            pltpu.VMEM((2, nx * ny - 1, 1, LANES), jnp.float32),
            pltpu.SemaphoreType.DMA((len(raw) + 1,)),
            pltpu.SemaphoreType.DMA((2, halo)),
            pltpu.SemaphoreType.DMA((2, halo)),
            pltpu.SemaphoreType.DMA((2, halo)),
            pltpu.SemaphoreType.DMA((2,)),
            pltpu.SemaphoreType.DMA((2, 2)),
        ],
        compiler_params=pltpu.CompilerParams(
            collective_id=0, has_side_effects=True, vmem_limit_bytes=24 * 1024 * 1024
        ),
        cost_estimate=pl.CostEstimate(
            flops=70 * pairs_kept, bytes_accessed=16 * width * SUBLANES, transcendentals=2 * pairs_kept
        ),
    )(tile_counts, *raw)
    return (jnp.swapaxes(current, 1, 2), weights)


def solution(mesh):
    cell_axes = P(("box", "gx"), "gy")
    return jax.shard_map(
        functools.partial(body, mesh.shape["gx"], mesh.shape["gy"]),
        mesh=mesh,
        in_specs=(cell_axes,) * 8,
        out_specs=(cell_axes, P("box")),
        check_vma=False,
    )
```
